32 devices in a mesh: role: 2 (over y), space: 4 (over z), freq: 4 (over x, core).
Axes of the slice: x: 2, y: 2, z: 4, core: 2. Of those that a mesh axis runs over, the one named last changes fastest.
Arguments:
- fields: float32 [2, 5, 8, 512], P('role', None, 'freq', 'space'), may hold values from -6 to 6
- spectra: float32 [2, 128, 4, 8, 512], P('role', 'freq', None, None, 'space'), may hold values from -6 to 6
- freq_index: int32 [128], P('freq'), may hold values from 1 to 63
- freq_weight: float32 [128], P('freq'), may hold values from 0.5 to 2
- material_ids: int32 [8, 512], P('freq', 'space'), may hold values from 0 to 7
- material: float32 [3, 8], replicated, may hold values from 0.5 to 2
- source_cells: int32 [2, 16], P('role'), may hold values from 0 to 4095
- wavelets: float32 [2, 8, 16], P('role'), may hold values from -6 to 6
Outputs:
- fields_out: float32 [2, 5, 8, 512], P('role', None, 'freq', 'space')
- spectra_out: float32 [2, 128, 4, 8, 512], P('role', 'freq', None, None, 'space')
- gradient: float32 [8, 512], P(('role', 'freq'), 'space')
The draws below stay inside these ranges and needn't reach their ends.
Inputs may be any that keep to these rules, and one draw needn't show every extreme that they name: `source_cells`: cells may repeat.
All inputs are finite; a program needn't handle non-finite values.
Results may differ from the reference program's by a relative error of at most 0.0033.
Values may be sent and summed in bfloat16 or wider, within the bound.
A program may use at most 64 MiB of HBM per device.

```python
import math
import jax
import jax.numpy as jnp
from jax import lax

F = 128
STEPS = 8
PERIOD = 64
NMAT = 8
NSRC = 16
NX = 8
NZ = 512


def touch_ends(array, stream_key, least, largest):
    longest = array.shape.index(max(array.shape))
    spots = []
    for shift in (0, 1):
        where = [jax.random.randint(jax.random.fold_in(stream_key, axis), (), 0, length) for axis, length in enumerate(array.shape)]
        where[longest] = (where[longest] + shift) % array.shape[longest]
        spots.append(tuple(where))
    return array.at[spots[0]].set(least).at[spots[1]].set(largest)


def levels(own_key, dims, cuts, low, high):
    def one(axis_at, parts):
        draws = jax.random.uniform(jax.random.fold_in(jax.random.fold_in(own_key, 6), axis_at), (parts,), jnp.float32, low / len(cuts), high / len(cuts))
        return jnp.repeat(jnp.exp(draws), dims[axis_at] // parts).reshape((-1,) + (1,) * (len(dims) - axis_at - 1))

    factor_of = one(*cuts[0])
    for cut in cuts[1:]:
        factor_of = factor_of * one(*cut)
    return factor_of


def scatter_about(stream_key, dims, scale, limit, cuts=(), kind=jnp.bfloat16):
    level = levels(stream_key, dims, cuts, -0.22, 0.18) if cuts else 1.0
    array = jax.random.normal(stream_key, dims, jnp.float32) * scale * level
    return jnp.minimum(jnp.maximum(array, -limit), limit).astype(kind)


def setup_inputs(seed: int = 0) -> dict:
    keys = jax.random.split(jax.random.key(seed), 9)
    fields = scatter_about(keys[0], (2, 5, NX, NZ), 1.0, 6.0, ((0, 2), (2, 4), (3, 4)), jnp.float32)
    spectra = scatter_about(keys[1], (2, F, 4, NX, NZ), 1.0, 6.0, ((0, 2), (1, 4), (4, 4)), jnp.float32)
    freq_index = touch_ends(jax.random.randint(keys[2], (F,), 1, PERIOD), jax.random.fold_in(keys[2], 1), 1, PERIOD - 1).astype(jnp.int32)
    freq_weight = jnp.clip(jnp.exp(math.log(2.0) - 1.3862944 * jax.random.uniform(keys[3], (F,), jnp.float32) ** levels(keys[3], (F,), ((0, 4),), -0.2, 0.2)), 0.5, 2.0)
    material_ids = touch_ends(jax.random.randint(keys[4], (NX, NZ), 0, NMAT), jax.random.fold_in(keys[4], 1), 0, NMAT - 1).astype(jnp.int32)
    material = jnp.clip(jnp.exp(jax.random.uniform(keys[5], (3, NMAT), jnp.float32, math.log(0.5), math.log(2.0))), 0.5, 2.0)
    source_cells = touch_ends(jax.random.randint(keys[6], (2, NSRC), 0, NX * NZ), jax.random.fold_in(keys[6], 1), 0, (NX * NZ) - 1).astype(jnp.int32)
    wavelets = scatter_about(keys[7], (2, STEPS, NSRC), 1.0, 6.0, ((0, 2),), jnp.float32)
    return {"fields": fields, "spectra": spectra, "freq_index": freq_index, "freq_weight": freq_weight, "material_ids": material_ids, "material": material, "source_cells": source_cells, "wavelets": wavelets}


COURANT = 0.18
TWO_PI = 6.283185307179586


def twiddle_table(freq_index):
    times = jnp.arange(STEPS, dtype=jnp.int32)
    turns = (freq_index[:, None] * times[None, :]) % PERIOD
    angle = turns.astype(jnp.float32) * (TWO_PI / PERIOD)
    table = jnp.stack([jnp.cos(angle), -jnp.sin(angle)], axis=1)
    return table.reshape(-1, STEPS).astype(jnp.bfloat16)


def velocity_update(velocity, padded, buoyancy):
    sigma_xx = padded[0, 1:-1, 1:-1]
    sigma_zz = padded[1, 1:-1, 1:-1]
    sigma_xz = padded[2, 1:-1, 1:-1]
    vel_x = velocity[0] + COURANT * buoyancy * ((padded[0, 2:, 1:-1] - sigma_xx) + (sigma_xz - padded[2, 1:-1, :-2]))
    vel_z = velocity[1] + COURANT * buoyancy * ((sigma_xz - padded[2, :-2, 1:-1]) + (padded[1, 1:-1, 2:] - sigma_zz))
    return jnp.stack([vel_x, vel_z])


def stress_update(stress, padded, lame_first, lame_second, inject):
    vel_x = padded[0, 1:-1, 1:-1]
    vel_z = padded[1, 1:-1, 1:-1]
    strain_x = vel_x - padded[0, :-2, 1:-1]
    strain_z = vel_z - padded[1, 1:-1, :-2]
    stiff = lame_first + 2.0 * lame_second
    sigma_xx = stress[0] + COURANT * (stiff * strain_x + lame_first * strain_z) + inject
    sigma_zz = stress[1] + COURANT * (lame_first * strain_x + stiff * strain_z) + inject
    sigma_xz = stress[2] + COURANT * lame_second * ((padded[0, 1:-1, 2:] - vel_x) + (padded[1, 2:, 1:-1] - vel_z))
    return jnp.stack([sigma_xx, sigma_zz, sigma_xz])


def reference(fields, spectra, freq_index, freq_weight, material_ids, material, source_cells, wavelets):
    props = material[:, material_ids]
    buoyancy, lame_first, lame_second = props[0], props[1], props[2]
    table = twiddle_table(freq_index)
    widths = ((0, 0), (1, 1), (1, 1))
    new_fields = []
    new_spectra = []
    for which in range(2):
        velocity = fields[which, :2]
        stress = fields[which, 2:]
        snaps = []
        for tick in range(STEPS):
            velocity = velocity_update(velocity, jnp.pad(stress, widths), buoyancy)
            flat = jnp.zeros((NX * NZ,), jnp.float32).at[source_cells[which]].add(wavelets[which, tick])
            stress = stress_update(stress, jnp.pad(velocity, widths), lame_first, lame_second, flat.reshape(NX, NZ))
            snaps.append(velocity.astype(jnp.bfloat16))
        stacked = jnp.stack(snaps).reshape(STEPS, -1)
        spectral = jnp.dot(table, stacked, preferred_element_type=jnp.float32).reshape(F, 4, NX, NZ)
        new_spectra.append(spectra[which] + spectral)
        new_fields.append(jnp.concatenate([velocity, stress], axis=0))
    forward, adjoint = new_spectra[0], new_spectra[1]

    def accumulate(index, total):
        return total + freq_weight[index] * jnp.sum(forward[index] * adjoint[index], axis=0)

    gradient = lax.fori_loop(0, F, accumulate, jnp.zeros((NX, NZ), jnp.float32)) / F
    return jnp.stack(new_fields), jnp.stack(new_spectra), gradient
```

```python
import functools
import math

import jax
import jax.numpy as jnp
from jax import lax
from jax.experimental import pallas as pl
from jax.experimental.pallas import tpu as pltpu
from jax.sharding import PartitionSpec as P

STEPS = 8
PERIOD = 64
COURANT = 0.18
TWO_PI = 6.283185307179586
PLANES = 6
MESH = pl.DeviceIdType.MESH


def log2(n):
    bits = n.bit_length() - 1
    assert n == 1 << bits
    return bits


def kernel(
    sizes,
    fields, ids, freq_index, freq_weight, material, cells, wavelets, spectra,
    fields_out, spectra_out, gradient,
    block, packed, center, halo, cells_far, wavelets_far, planes, edges,
    inject_left, inject, table, snaps, spectrum, bulk, bulk_far, final, sums, sums_far,
    center_send, center_recv, halo_send, halo_recv, small_send, small_recv,
    bulk_send, bulk_recv, sums_send, sums_recv, load_sem, store_sem,
):
    groups, spaces, local_freqs, rows, columns = sizes
    count = 2 * groups
    rows_all = rows * groups
    span = 2 * STEPS
    wide = 2 * columns
    half = local_freqs // 2
    nmat = material.shape[1]
    nsrc = cells.shape[1]
    role = lax.axis_index("role")
    space = lax.axis_index("space")
    group = lax.axis_index("freq")
    other = 1 - role
    me = role * groups + group

    def device(index, at):
        return {"role": index // groups, "space": at, "freq": index % groups}

    def peer(step):
        return lax.rem(me + step, count)

    has_low = space > 0
    has_high = space < spaces - 1

    halo[...] = jnp.zeros_like(halo)

    barrier = pltpu.get_barrier_semaphore()

    @pl.when(has_low)
    def _():
        for step in range(count):
            pl.semaphore_signal(barrier, inc=1, device_id=device(peer(step), space - 1), device_id_type=MESH)

    @pl.when(has_high)
    def _():
        for step in range(count):
            pl.semaphore_signal(barrier, inc=1, device_id=device(peer(step), space + 1), device_id_type=MESH)

    for step in range(1, count):
        pl.semaphore_signal(barrier, inc=1, device_id=device(peer(step), space), device_id_type=MESH)

    away = pl.ds(other * half, half)
    home = pl.ds(role * half, half)
    load_away = pltpu.make_async_copy(spectra.at[0, away], spectrum.at[away], load_sem.at[0])
    load_home = pltpu.make_async_copy(spectra.at[0, home], spectrum.at[home], load_sem.at[1])
    load_away.start()
    load_home.start()

    for plane in range(PLANES - 1):
        block[plane] = fields[0, plane]
    block[PLANES - 1] = (ids[...] + 1).astype(jnp.float32)
    lane = lax.broadcasted_iota(jnp.int32, (rows, columns), 1)
    pack = jnp.zeros((rows, columns), jnp.float32)
    for plane in range(PLANES):
        value = block[plane]
        if plane:
            value = pltpu.roll(value, span * plane, 1)
        place = (lane - (span * plane - STEPS)) & (columns - 1)
        pack = jnp.where(place < span, value, pack)
    packed[...] = pack

    beside = lax.div(space + spaces - 1, spaces) + lax.div(2 * spaces - 2 - space, spaces)
    pl.semaphore_wait(barrier, count - 1 + count * beside)

    def halo_copy(side, step, at, slot):
        return pltpu.make_async_remote_copy(
            src_ref=packed, dst_ref=halo.at[side, slot],
            send_sem=halo_send.at[side, step], recv_sem=halo_recv.at[side, slot],
            device_id=device(peer(step), at), device_id_type=MESH,
        )

    def center_copy(step, slot):
        return pltpu.make_async_remote_copy(
            src_ref=block, dst_ref=center.at[slot],
            send_sem=center_send.at[step], recv_sem=center_recv.at[slot],
            device_id=device(peer(step), space), device_id_type=MESH,
        )

    partner = {"role": other, "space": space, "freq": group}
    cells_copy = pltpu.make_async_remote_copy(
        src_ref=cells, dst_ref=cells_far, send_sem=small_send.at[0], recv_sem=small_recv.at[0],
        device_id=partner, device_id_type=MESH,
    )
    wavelets_copy = pltpu.make_async_remote_copy(
        src_ref=wavelets, dst_ref=wavelets_far, send_sem=small_send.at[1], recv_sem=small_recv.at[1],
        device_id=partner, device_id_type=MESH,
    )
    bulk_copy = pltpu.make_async_remote_copy(
        src_ref=bulk, dst_ref=bulk_far, send_sem=bulk_send, recv_sem=bulk_recv,
        device_id=partner, device_id_type=MESH,
    )

    @pl.when(has_high)
    def _():
        for step in range(count):
            halo_copy(0, step, space + 1, me).start()

    @pl.when(has_low)
    def _():
        for step in range(count):
            halo_copy(1, step, space - 1, me).start()

    for step in range(1, count):
        center_copy(step, me).start()
    cells_copy.start()
    wavelets_copy.start()

    load_away.wait()
    for index in range(half):
        bulk[index] = spectrum[other * half + index].reshape(4 * rows_all, columns).astype(jnp.bfloat16)
    bulk_copy.start()

    depth = 2 * STEPS * rows_all
    at_row = lax.broadcasted_iota(jnp.int32, (2 * rows_all, depth), 0)
    at_lane = lax.broadcasted_iota(jnp.int32, (2 * rows_all, depth), 1)
    step_of = (at_lane >> log2(rows_all)) & (STEPS - 1)
    turn = jnp.where(at_lane >= STEPS * rows_all, PERIOD // 4, 0)
    match = (at_lane & (rows_all - 1)) == (at_row & (rows_all - 1))
    for pair in range(local_freqs // 2):
        number = jnp.where(at_row < rows_all, freq_index[2 * pair], freq_index[2 * pair + 1])
        turns = (number * step_of + turn) & (PERIOD - 1)
        value = jnp.cos(turns.astype(jnp.float32) * (TWO_PI / PERIOD))
        table[pl.ds(pair * 2 * rows_all, 2 * rows_all), :] = jnp.where(match, value, 0.0).astype(jnp.bfloat16)

    def injection(which, cell_row, wavelet_rows):
        cell_at = jnp.broadcast_to(cell_row, (rows_all, nsrc)) >> log2(columns * spaces)
        row_at = lax.broadcasted_iota(jnp.int32, (rows_all, nsrc), 0)
        for tick in range(STEPS):
            amount = jnp.broadcast_to(wavelet_rows[tick:tick + 1, :], (rows_all, nsrc))
            inject_left[pl.ds(tick * rows_all, rows_all), :] = jnp.where(cell_at == row_at, amount, 0.0)
        column_at = lax.broadcasted_iota(jnp.int32, (wide, nsrc), 0)
        shift = jnp.where(column_at >= wide - STEPS, column_at - wide, column_at) + space * columns
        shift = jnp.where((column_at >= columns + STEPS) & (column_at < wide - STEPS), -1, shift)
        wanted = jnp.broadcast_to(cell_row, (wide, nsrc)) & (columns * spaces - 1)
        hit = (shift == wanted).astype(jnp.float32)
        inject[which] = lax.dot_general(
            inject_left[...], hit, (((1,), (1,)), ((), ())),
            precision=lax.Precision.HIGHEST, preferred_element_type=jnp.float32,
        )

    injection(0, cells[...], wavelets[0])

    cells_copy.wait_recv()
    wavelets_copy.wait_recv()
    injection(1, cells_far[...], wavelets_far[0])

    for step in range(1, count):
        center_copy(step, peer(step)).wait_recv()
    for plane in range(PLANES):
        center[me, plane] = block[plane]

    for which, owner in ((0, role), (1, other)):
        for part in range(groups):
            slot = owner * groups + part
            for plane in range(PLANES):
                planes[which, plane, pl.ds(part * rows, rows), :] = center[slot, plane]

    @pl.when(has_low)
    def _():
        for step in range(count):
            halo_copy(0, step, space - 1, peer(step)).wait_recv()

    @pl.when(has_high)
    def _():
        for step in range(count):
            halo_copy(1, step, space + 1, peer(step)).wait_recv()

    low_part = (lane & (span - 1)) < STEPS
    for which, owner in ((0, role), (1, other)):
        for part in range(groups):
            slot = owner * groups + part
            edges[which, pl.ds(part * rows, rows), :] = jnp.where(low_part, halo[1, slot], halo[0, slot])

    lane_all = lax.broadcasted_iota(jnp.int32, (rows_all, columns), 1)
    rim = (lane_all < STEPS) | (lane_all >= columns - STEPS)

    def whole(which, plane):
        outer = edges[which]
        if plane:
            outer = pltpu.roll(outer, columns - span * plane, 1)
        return jnp.concatenate([planes[which, plane], jnp.where(rim, outer, 0.0)], axis=1)

    ident = whole(0, PLANES - 1)
    props = [jnp.zeros_like(ident) for _ in range(3)]
    for block_id in range(nmat):
        same = ident == float(block_id + 1)
        props = [jnp.where(same, material[k, block_id], props[k]) for k in range(3)]
    buoyancy = COURANT * props[0]
    first = COURANT * props[1]
    second = COURANT * props[2]
    stiff = first + 2.0 * second

    row_id = lax.broadcasted_iota(jnp.int32, (rows_all, wide), 0)
    not_top = row_id > 0
    not_end = row_id < rows_all - 1

    def up(x):
        return jnp.where(not_end, pltpu.roll(x, rows_all - 1, 0), 0.0)

    def down(x):
        return jnp.where(not_top, pltpu.roll(x, 1, 0), 0.0)

    def right(x):
        return pltpu.roll(x, wide - 1, 1)

    def left(x):
        return pltpu.roll(x, 1, 1)

    state = [[whole(which, plane) for plane in range(5)] for which in range(2)]
    for tick in range(STEPS):
        at = pl.ds(tick * rows_all, rows_all)
        for which in range(2):
            vx, vz, xx, zz, xz = state[which]
            vx = vx + buoyancy * ((up(xx) - xx) + (xz - left(xz)))
            vz = vz + buoyancy * ((xz - down(xz)) + (right(zz) - zz))
            source = inject[which, at, :]
            ex = vx - down(vx)
            ez = vz - left(vz)
            xx = xx + (stiff * ex + first * ez) + source
            zz = zz + (first * ex + stiff * ez) + source
            xz = xz + second * ((right(vx) - vx) + (up(vz) - vz))
            state[which] = [vx, vz, xx, zz, xz]
            snaps[which, at, 0:columns] = vx[:, :columns]
            snaps[which, at, columns:wide] = vz[:, :columns]
    for plane in range(5):
        final[plane] = state[0][plane][:, :columns]
    for plane in range(5):
        fields_out[0, plane] = final[plane, pl.ds(group * rows, rows), :]

    def right_side(which):
        snap = snaps[which].astype(jnp.bfloat16)
        zero = jnp.zeros_like(snap)
        return jnp.concatenate(
            [jnp.concatenate([snap, zero], axis=1), jnp.concatenate([zero, snap], axis=1)], axis=0
        )

    def products(which_freqs, side):
        lines = pl.ds(pl.multiple_of(which_freqs * half * rows_all, 16), half * rows_all)
        return jnp.dot(table[lines, :], side, preferred_element_type=jnp.float32)

    def piece(value, index, part):
        return value[index * rows_all:(index + 1) * rows_all, part * columns:(part + 1) * columns]

    load_home.wait()
    side = right_side(0)
    near = products(role, side)
    far = products(role, right_side(1))
    bulk_copy.wait_recv()
    total = jnp.zeros((rows_all, columns), jnp.float32)
    for index in range(half):
        theirs = bulk_far[index].astype(jnp.float32)
        term = jnp.zeros((rows_all, columns), jnp.float32)
        for part in range(4):
            mine = spectrum[role * half + index, part] + piece(near, index, part)
            spectrum[role * half + index, part] = mine
            term = term + mine * (theirs[part * rows_all:(part + 1) * rows_all] + piece(far, index, part))
        total = total + freq_weight[role * half + index] * term
    total = total * (1.0 / (local_freqs * groups))
    each = rows_all // count
    for slot in range(count):
        sums[slot] = total[slot * each:(slot + 1) * each]

    def sums_copy(step, slot):
        return pltpu.make_async_remote_copy(
            src_ref=sums.at[peer(step)], dst_ref=sums_far.at[slot],
            send_sem=sums_send.at[step], recv_sem=sums_recv.at[slot],
            device_id=device(peer(step), space), device_id_type=MESH,
        )

    for step in range(1, count):
        sums_copy(step, me).start()
    store_home = pltpu.make_async_copy(spectrum.at[home], spectra_out.at[0, home], store_sem.at[0])
    store_home.start()

    rest = products(other, side)
    for index in range(half):
        for part in range(4):
            spectrum[other * half + index, part] = spectrum[other * half + index, part] + piece(rest, index, part)
    store_away = pltpu.make_async_copy(spectrum.at[away], spectra_out.at[0, away], store_sem.at[1])
    store_away.start()

    answer = sums[me]
    for step in range(1, count):
        sums_copy(step, peer(step)).wait_recv()
        answer = answer + sums_far[peer(step)]
    gradient[...] = answer

    @pl.when(has_high)
    def _():
        for step in range(count):
            halo_copy(0, step, space + 1, me).wait_send()

    @pl.when(has_low)
    def _():
        for step in range(count):
            halo_copy(1, step, space - 1, me).wait_send()

    for step in range(1, count):
        center_copy(step, me).wait_send()
        sums_copy(step, me).wait_send()
    cells_copy.wait_send()
    wavelets_copy.wait_send()
    bulk_copy.wait_send()
    store_home.wait()
    store_away.wait()


def local(fields, spectra, freq_index, freq_weight, material_ids, material, source_cells, wavelets):
    groups = lax.axis_size("freq")
    spaces = lax.axis_size("space")
    rows, columns = fields.shape[2:]
    local_freqs = freq_index.shape[0]
    rows_all = rows * groups
    count = 2 * groups
    half = local_freqs // 2
    nsrc = source_cells.shape[1]
    wide = 2 * columns
    sizes = (groups, spaces, local_freqs, rows, columns)
    f32 = jnp.float32
    vmem = pl.BlockSpec(memory_space=pltpu.VMEM)
    smem = pl.BlockSpec(memory_space=pltpu.SMEM)
    anywhere = pl.BlockSpec(memory_space=pl.ANY)
    dma = pltpu.SemaphoreType.DMA
    return tuple(pl.pallas_call(
        functools.partial(kernel, sizes),
        out_shape=(
            jax.ShapeDtypeStruct(fields.shape, f32),
            jax.ShapeDtypeStruct(spectra.shape, f32),
            jax.ShapeDtypeStruct((rows_all // count, columns), f32),
        ),
        in_specs=[vmem, vmem, smem, smem, smem, vmem, vmem, anywhere],
        out_specs=(vmem, anywhere, vmem),
        scratch_shapes=[
            pltpu.VMEM((PLANES, rows, columns), f32),
            pltpu.VMEM((rows, columns), f32),
            pltpu.VMEM((count, PLANES, rows, columns), f32),
            pltpu.VMEM((2, count, rows, columns), f32),
            pltpu.VMEM((1, nsrc), jnp.int32),
            pltpu.VMEM((1, STEPS, nsrc), f32),
            pltpu.VMEM((2, PLANES, rows_all, columns), f32),
            pltpu.VMEM((2, rows_all, columns), f32),
            pltpu.VMEM((STEPS * rows_all, nsrc), f32),
            pltpu.VMEM((2, STEPS * rows_all, wide), f32),
            pltpu.VMEM((local_freqs * rows_all, 2 * STEPS * rows_all), jnp.bfloat16),
            pltpu.VMEM((2, STEPS * rows_all, wide), f32),
            pltpu.VMEM((local_freqs, 4, rows_all, columns), f32),
            pltpu.VMEM((half, 4 * rows_all, columns), jnp.bfloat16),
            pltpu.VMEM((half, 4 * rows_all, columns), jnp.bfloat16),
            pltpu.VMEM((5, rows_all, columns), f32),
            pltpu.VMEM((count, rows_all // count, columns), f32),
            pltpu.VMEM((count, rows_all // count, columns), f32),
            dma((count,)), dma((count,)), dma((2, count)), dma((2, count)), dma((2,)), dma((2,)),
            dma, dma, dma((count,)), dma((count,)), dma((2,)), dma((2,)),
        ],
        compiler_params=pltpu.CompilerParams(collective_id=0, has_side_effects=True),
    )(fields, material_ids, freq_index, freq_weight, material, source_cells, wavelets, spectra))


def solution(mesh):
    return jax.shard_map(
        local,
        mesh=mesh,
        in_specs=(
            P("role", None, "freq", "space"),
            P("role", "freq", None, None, "space"),
            P("freq"),
            P("freq"),
            P("freq", "space"),
            P(),
            P("role", None),
            P("role", None, None),
        ),
        out_specs=(
            P("role", None, "freq", "space"),
            P("role", "freq", None, None, "space"),
            P(("role", "freq"), "space"),
        ),
        check_vma=False,
    )
```

```python
import functools
import math

import jax
import jax.numpy as jnp
from jax import lax
from jax.experimental import pallas as pl
from jax.experimental.pallas import tpu as pltpu
from jax.sharding import PartitionSpec as P

STEPS = 8
PERIOD = 64
COURANT = 0.18
TWO_PI = 6.283185307179586
PLANES = 6
MESH = pl.DeviceIdType.MESH


def log2(n):
    bits = n.bit_length() - 1
    assert n == 1 << bits
    return bits


def kernel(
    sizes,
    fields, ids, freq_index, freq_weight, material, cells, wavelets, spectra,
    fields_out, spectrum, gradient,
    block, packed, center, halo, cells_far, wavelets_far, planes, edges,
    inject_left, inject, table, snaps, bulk, bulk_far, final, sums, sums_far,
    center_send, center_recv, halo_send, halo_recv, small_send, small_recv,
    bulk_send, bulk_recv, sums_send, sums_recv, load_sem,
):
    groups, spaces, local_freqs, rows, columns = sizes
    count = 2 * groups
    rows_all = rows * groups
    span = 2 * STEPS
    wide = 2 * columns
    half = local_freqs // 2
    nmat = material.shape[1]
    nsrc = cells.shape[1]
    role = lax.axis_index("role")
    space = lax.axis_index("space")
    group = lax.axis_index("freq")
    other = 1 - role
    me = role * groups + group

    def device(index, at):
        return {"role": index // groups, "space": at, "freq": index % groups}

    def peer(step):
        return lax.rem(me + step, count)

    has_low = space > 0
    has_high = space < spaces - 1

    halo[...] = jnp.zeros_like(halo)

    barrier = pltpu.get_barrier_semaphore()

    @pl.when(has_low)
    def _():
        for step in range(count):
            pl.semaphore_signal(barrier, inc=1, device_id=device(peer(step), space - 1), device_id_type=MESH)

    @pl.when(has_high)
    def _():
        for step in range(count):
            pl.semaphore_signal(barrier, inc=1, device_id=device(peer(step), space + 1), device_id_type=MESH)

    for step in range(1, count):
        pl.semaphore_signal(barrier, inc=1, device_id=device(peer(step), space), device_id_type=MESH)

    away = pl.ds(other * half, half)
    home = pl.ds(role * half, half)
    load_away = pltpu.make_async_copy(spectra.at[0, away], spectrum.at[away], load_sem.at[0])
    load_home = pltpu.make_async_copy(spectra.at[0, home], spectrum.at[home], load_sem.at[1])
    load_away.start()
    load_home.start()

    for plane in range(PLANES - 1):
        block[plane] = fields[0, plane]
    block[PLANES - 1] = (ids[...] + 1).astype(jnp.float32)
    lane = lax.broadcasted_iota(jnp.int32, (rows, columns), 1)
    pack = jnp.zeros((rows, columns), jnp.float32)
    for plane in range(PLANES):
        value = block[plane]
        if plane:
            value = pltpu.roll(value, span * plane, 1)
        place = (lane - (span * plane - STEPS)) & (columns - 1)
        pack = jnp.where(place < span, value, pack)
    packed[...] = pack

    beside = lax.div(space + spaces - 1, spaces) + lax.div(2 * spaces - 2 - space, spaces)
    pl.semaphore_wait(barrier, count - 1 + count * beside)

    def halo_copy(side, step, at, slot):
        return pltpu.make_async_remote_copy(
            src_ref=packed, dst_ref=halo.at[side, slot],
            send_sem=halo_send.at[side, step], recv_sem=halo_recv.at[side, slot],
            device_id=device(peer(step), at), device_id_type=MESH,
        )

    def center_copy(step, slot):
        return pltpu.make_async_remote_copy(
            src_ref=block, dst_ref=center.at[slot],
            send_sem=center_send.at[step], recv_sem=center_recv.at[slot],
            device_id=device(peer(step), space), device_id_type=MESH,
        )

    partner = {"role": other, "space": space, "freq": group}
    cells_copy = pltpu.make_async_remote_copy(
        src_ref=cells, dst_ref=cells_far, send_sem=small_send.at[0], recv_sem=small_recv.at[0],
        device_id=partner, device_id_type=MESH,
    )
    wavelets_copy = pltpu.make_async_remote_copy(
        src_ref=wavelets, dst_ref=wavelets_far, send_sem=small_send.at[1], recv_sem=small_recv.at[1],
        device_id=partner, device_id_type=MESH,
    )
    bulk_copy = pltpu.make_async_remote_copy(
        src_ref=bulk, dst_ref=bulk_far, send_sem=bulk_send, recv_sem=bulk_recv,
        device_id=partner, device_id_type=MESH,
    )

    @pl.when(has_high)
    def _():
        for step in range(count):
            halo_copy(0, step, space + 1, me).start()

    @pl.when(has_low)
    def _():
        for step in range(count):
            halo_copy(1, step, space - 1, me).start()

    for step in range(1, count):
        center_copy(step, me).start()
    cells_copy.start()
    wavelets_copy.start()

    load_away.wait()
    for index in range(half):
        bulk[index] = spectrum[other * half + index].reshape(4 * rows_all, columns).astype(jnp.bfloat16)
    bulk_copy.start()

    depth = 2 * STEPS * rows_all
    at_row = lax.broadcasted_iota(jnp.int32, (2 * rows_all, depth), 0)
    at_lane = lax.broadcasted_iota(jnp.int32, (2 * rows_all, depth), 1)
    step_of = (at_lane >> log2(rows_all)) & (STEPS - 1)
    turn = jnp.where(at_lane >= STEPS * rows_all, PERIOD // 4, 0)
    match = (at_lane & (rows_all - 1)) == (at_row & (rows_all - 1))
    for pair in range(local_freqs // 2):
        number = jnp.where(at_row < rows_all, freq_index[2 * pair], freq_index[2 * pair + 1])
        turns = (number * step_of + turn) & (PERIOD - 1)
        value = jnp.cos(turns.astype(jnp.float32) * (TWO_PI / PERIOD))
        table[pl.ds(pair * 2 * rows_all, 2 * rows_all), :] = jnp.where(match, value, 0.0).astype(jnp.bfloat16)

    def injection(which, cell_row, wavelet_rows):
        cell_at = jnp.broadcast_to(cell_row, (rows_all, nsrc)) >> log2(columns * spaces)
        row_at = lax.broadcasted_iota(jnp.int32, (rows_all, nsrc), 0)
        for tick in range(STEPS):
            amount = jnp.broadcast_to(wavelet_rows[tick:tick + 1, :], (rows_all, nsrc))
            inject_left[pl.ds(tick * rows_all, rows_all), :] = jnp.where(cell_at == row_at, amount, 0.0)
        column_at = lax.broadcasted_iota(jnp.int32, (wide, nsrc), 0)
        shift = jnp.where(column_at >= wide - STEPS, column_at - wide, column_at) + space * columns
        shift = jnp.where((column_at >= columns + STEPS) & (column_at < wide - STEPS), -1, shift)
        wanted = jnp.broadcast_to(cell_row, (wide, nsrc)) & (columns * spaces - 1)
        hit = (shift == wanted).astype(jnp.float32)
        inject[which] = lax.dot_general(
            inject_left[...], hit, (((1,), (1,)), ((), ())),
            precision=lax.Precision.HIGHEST, preferred_element_type=jnp.float32,
        )

    injection(0, cells[...], wavelets[0])

    cells_copy.wait_recv()
    wavelets_copy.wait_recv()
    injection(1, cells_far[...], wavelets_far[0])

    for step in range(1, count):
        center_copy(step, peer(step)).wait_recv()
    for plane in range(PLANES):
        center[me, plane] = block[plane]

    for which, owner in ((0, role), (1, other)):
        for part in range(groups):
            slot = owner * groups + part
            for plane in range(PLANES):
                planes[which, plane, pl.ds(part * rows, rows), :] = center[slot, plane]

    @pl.when(has_low)
    def _():
        for step in range(count):
            halo_copy(0, step, space - 1, peer(step)).wait_recv()

    @pl.when(has_high)
    def _():
        for step in range(count):
            halo_copy(1, step, space + 1, peer(step)).wait_recv()

    low_part = (lane & (span - 1)) < STEPS
    for which, owner in ((0, role), (1, other)):
        for part in range(groups):
            slot = owner * groups + part
            edges[which, pl.ds(part * rows, rows), :] = jnp.where(low_part, halo[1, slot], halo[0, slot])

    lane_all = lax.broadcasted_iota(jnp.int32, (rows_all, columns), 1)
    rim = (lane_all < STEPS) | (lane_all >= columns - STEPS)

    def whole(which, plane):
        outer = edges[which]
        if plane:
            outer = pltpu.roll(outer, columns - span * plane, 1)
        return jnp.concatenate([planes[which, plane], jnp.where(rim, outer, 0.0)], axis=1)

    ident = whole(0, PLANES - 1)
    props = [jnp.zeros_like(ident) for _ in range(3)]
    for block_id in range(nmat):
        same = ident == float(block_id + 1)
        props = [jnp.where(same, material[k, block_id], props[k]) for k in range(3)]
    buoyancy = COURANT * props[0]
    first = COURANT * props[1]
    second = COURANT * props[2]
    stiff = first + 2.0 * second

    row_id = lax.broadcasted_iota(jnp.int32, (rows_all, wide), 0)
    not_top = row_id > 0
    not_end = row_id < rows_all - 1

    def up(x):
        return jnp.where(not_end, pltpu.roll(x, rows_all - 1, 0), 0.0)

    def down(x):
        return jnp.where(not_top, pltpu.roll(x, 1, 0), 0.0)

    def right(x):
        return pltpu.roll(x, wide - 1, 1)

    def left(x):
        return pltpu.roll(x, 1, 1)

    state = [[whole(which, plane) for plane in range(5)] for which in range(2)]
    for tick in range(STEPS):
        at = pl.ds(tick * rows_all, rows_all)
        for which in range(2):
            vx, vz, xx, zz, xz = state[which]
            vx = vx + buoyancy * ((up(xx) - xx) + (xz - left(xz)))
            vz = vz + buoyancy * ((xz - down(xz)) + (right(zz) - zz))
            source = inject[which, at, :]
            ex = vx - down(vx)
            ez = vz - left(vz)
            xx = xx + (stiff * ex + first * ez) + source
            zz = zz + (first * ex + stiff * ez) + source
            xz = xz + second * ((right(vx) - vx) + (up(vz) - vz))
            state[which] = [vx, vz, xx, zz, xz]
            snaps[which, at, 0:columns] = vx[:, :columns]
            snaps[which, at, columns:wide] = vz[:, :columns]
    for plane in range(5):
        final[plane] = state[0][plane][:, :columns]
    for plane in range(5):
        fields_out[0, plane] = final[plane, pl.ds(group * rows, rows), :]

    def right_side(which):
        snap = snaps[which].astype(jnp.bfloat16)
        zero = jnp.zeros_like(snap)
        return jnp.concatenate(
            [jnp.concatenate([snap, zero], axis=1), jnp.concatenate([zero, snap], axis=1)], axis=0
        )

    def products(which_freqs, side):
        lines = pl.ds(pl.multiple_of(which_freqs * half * rows_all, 16), half * rows_all)
        return jnp.dot(table[lines, :], side, preferred_element_type=jnp.float32)

    def piece(value, index, part):
        return value[index * rows_all:(index + 1) * rows_all, part * columns:(part + 1) * columns]

    load_home.wait()
    side = right_side(0)
    near = products(role, side)
    far = products(role, right_side(1))
    bulk_copy.wait_recv()
    total = jnp.zeros((rows_all, columns), jnp.float32)
    for index in range(half):
        theirs = bulk_far[index].astype(jnp.float32)
        term = jnp.zeros((rows_all, columns), jnp.float32)
        for part in range(4):
            mine = spectrum[role * half + index, part] + piece(near, index, part)
            spectrum[role * half + index, part] = mine
            term = term + mine * (theirs[part * rows_all:(part + 1) * rows_all] + piece(far, index, part))
        total = total + freq_weight[role * half + index] * term
    total = total * (1.0 / (local_freqs * groups))
    each = rows_all // count
    for slot in range(count):
        sums[slot] = total[slot * each:(slot + 1) * each]

    def sums_copy(step, slot):
        return pltpu.make_async_remote_copy(
            src_ref=sums.at[peer(step)], dst_ref=sums_far.at[slot],
            send_sem=sums_send.at[step], recv_sem=sums_recv.at[slot],
            device_id=device(peer(step), space), device_id_type=MESH,
        )

    for step in range(1, count):
        sums_copy(step, me).start()
    rest = products(other, side)
    for index in range(half):
        for part in range(4):
            spectrum[other * half + index, part] = spectrum[other * half + index, part] + piece(rest, index, part)

    answer = sums[me]
    for step in range(1, count):
        sums_copy(step, peer(step)).wait_recv()
        answer = answer + sums_far[peer(step)]
    gradient[...] = answer

    @pl.when(has_high)
    def _():
        for step in range(count):
            halo_copy(0, step, space + 1, me).wait_send()

    @pl.when(has_low)
    def _():
        for step in range(count):
            halo_copy(1, step, space - 1, me).wait_send()

    for step in range(1, count):
        center_copy(step, me).wait_send()
        sums_copy(step, me).wait_send()
    cells_copy.wait_send()
    wavelets_copy.wait_send()
    bulk_copy.wait_send()


def deliver(fields, spectrum, gradient, fields_out, spectra_out, gradient_out, sem):
    copies = [
        pltpu.make_async_copy(spectrum, spectra_out.at[0], sem.at[0]),
        pltpu.make_async_copy(fields, fields_out, sem.at[1]),
        pltpu.make_async_copy(gradient, gradient_out, sem.at[2]),
    ]
    for copy in copies:
        copy.start()
    for copy in copies:
        copy.wait()


def local(fields, spectra, freq_index, freq_weight, material_ids, material, source_cells, wavelets):
    groups = lax.axis_size("freq")
    spaces = lax.axis_size("space")
    rows, columns = fields.shape[2:]
    local_freqs = freq_index.shape[0]
    rows_all = rows * groups
    count = 2 * groups
    half = local_freqs // 2
    nsrc = source_cells.shape[1]
    wide = 2 * columns
    sizes = (groups, spaces, local_freqs, rows, columns)
    f32 = jnp.float32
    vmem = pl.BlockSpec(memory_space=pltpu.VMEM)
    smem = pl.BlockSpec(memory_space=pltpu.SMEM)
    anywhere = pl.BlockSpec(memory_space=pl.ANY)
    dma = pltpu.SemaphoreType.DMA
    results = pl.pallas_call(
        functools.partial(kernel, sizes),
        out_shape=(
            pltpu.VMEM(fields.shape, f32),
            pltpu.VMEM(spectra.shape[1:], f32),
            pltpu.VMEM((rows_all // count, columns), f32),
        ),
        in_specs=[vmem, vmem, smem, smem, smem, vmem, vmem, anywhere],
        out_specs=(vmem, vmem, vmem),
        scratch_shapes=[
            pltpu.VMEM((PLANES, rows, columns), f32),
            pltpu.VMEM((rows, columns), f32),
            pltpu.VMEM((count, PLANES, rows, columns), f32),
            pltpu.VMEM((2, count, rows, columns), f32),
            pltpu.VMEM((1, nsrc), jnp.int32),
            pltpu.VMEM((1, STEPS, nsrc), f32),
            pltpu.VMEM((2, PLANES, rows_all, columns), f32),
            pltpu.VMEM((2, rows_all, columns), f32),
            pltpu.VMEM((STEPS * rows_all, nsrc), f32),
            pltpu.VMEM((2, STEPS * rows_all, wide), f32),
            pltpu.VMEM((local_freqs * rows_all, 2 * STEPS * rows_all), jnp.bfloat16),
            pltpu.VMEM((2, STEPS * rows_all, wide), f32),
            pltpu.VMEM((half, 4 * rows_all, columns), jnp.bfloat16),
            pltpu.VMEM((half, 4 * rows_all, columns), jnp.bfloat16),
            pltpu.VMEM((5, rows_all, columns), f32),
            pltpu.VMEM((count, rows_all // count, columns), f32),
            pltpu.VMEM((count, rows_all // count, columns), f32),
            dma((count,)), dma((count,)), dma((2, count)), dma((2, count)), dma((2,)), dma((2,)),
            dma, dma, dma((count,)), dma((count,)), dma((2,)),
        ],
        compiler_params=pltpu.CompilerParams(collective_id=0, has_side_effects=True),
    )(fields, material_ids, freq_index, freq_weight, material, source_cells, wavelets, spectra)
    return tuple(pl.pallas_call(
        deliver,
        out_shape=(
            jax.ShapeDtypeStruct(fields.shape, f32),
            jax.ShapeDtypeStruct(spectra.shape, f32),
            jax.ShapeDtypeStruct((rows_all // count, columns), f32),
        ),
        in_specs=[vmem, vmem, vmem],
        out_specs=(anywhere, anywhere, anywhere),
        scratch_shapes=[dma((3,))],
    )(*[pltpu.with_memory_space_constraint(x, pltpu.VMEM) for x in results]))


def solution(mesh):
    return jax.shard_map(
        local,
        mesh=mesh,
        in_specs=(
            P("role", None, "freq", "space"),
            P("role", "freq", None, None, "space"),
            P("freq"),
            P("freq"),
            P("freq", "space"),
            P(),
            P("role", None),
            P("role", None, None),
        ),
        out_specs=(
            P("role", None, "freq", "space"),
            P("role", "freq", None, None, "space"),
            P(("role", "freq"), "space"),
        ),
        check_vma=False,
    )
```

```python
import functools
import math

import jax
import jax.numpy as jnp
from jax import lax
from jax.experimental import pallas as pl
from jax.experimental.pallas import tpu as pltpu
from jax.sharding import PartitionSpec as P

STEPS = 8
PERIOD = 64
COURANT = 0.18
TWO_PI = 6.283185307179586
PLANES = 6
PIECES = 8
MESH = pl.DeviceIdType.MESH


def log2(n):
    bits = n.bit_length() - 1
    assert n == 1 << bits
    return bits


def kernel(
    sizes,
    fields_in, ids_in, freq_index_in, freq_weight_in, material_in, cells_in, wavelets_in, spectra,
    fields_out, spectrum, gradient,
    ids, freq_index, freq_weight, material, cells, wavelets,
    block, packed, center, halo, cells_far, wavelets_far, planes, edges,
    inject_left, inject, table, snaps, bulk, bulk_far, final, sums, sums_far,
    center_send, center_recv, halo_send, halo_recv, small_send, small_recv,
    bulk_send, bulk_recv, sums_send, sums_recv, load_sem, input_sem,
):
    groups, spaces, local_freqs, rows, columns = sizes
    count = 2 * groups
    rows_all = rows * groups
    span = 2 * STEPS
    wide = 2 * columns
    half = local_freqs // 2
    nmat = material.shape[1]
    nsrc = cells.shape[1]
    role = lax.axis_index("role")
    space = lax.axis_index("space")
    group = lax.axis_index("freq")
    other = 1 - role
    me = role * groups + group

    places = []
    for flip in (role, other):
        for step in range(groups):
            places.append((flip, lax.rem(group + step, groups)))
    slots = [flip * groups + at for flip, at in places]

    def device(step, at):
        return {"role": places[step][0], "space": at, "freq": places[step][1]}

    def peer(step):
        return slots[step]

    away = pl.ds(other * half, half)
    home = pl.ds(role * half, half)
    load_away = pltpu.make_async_copy(spectra.at[0, away], spectrum.at[away], load_sem.at[0])
    load_home = pltpu.make_async_copy(spectra.at[0, home], spectrum.at[home], load_sem.at[1])
    inputs = [
        pltpu.make_async_copy(source, target, input_sem.at[index])
        for index, (source, target) in enumerate((
            (fields_in.at[0], block.at[pl.ds(0, PLANES - 1)]), (ids_in, ids), (cells_in, cells),
            (wavelets_in, wavelets), (freq_index_in, freq_index), (material_in, material),
            (freq_weight_in, freq_weight),
        ))
    ]

    has_low = space > 0
    has_high = space < spaces - 1

    for copy in inputs:
        copy.start()

    halo[...] = jnp.zeros_like(halo)

    barrier = pltpu.get_barrier_semaphore()

    @pl.when(has_low)
    def _():
        for step in range(count):
            pl.semaphore_signal(barrier, inc=1, device_id=device(step, space - 1), device_id_type=MESH)

    @pl.when(has_high)
    def _():
        for step in range(count):
            pl.semaphore_signal(barrier, inc=1, device_id=device(step, space + 1), device_id_type=MESH)

    for step in range(1, count):
        pl.semaphore_signal(barrier, inc=1, device_id=device(step, space), device_id_type=MESH)

    load_away.start()
    load_home.start()
    for copy in inputs[:2]:
        copy.wait()

    block[PLANES - 1] = (ids[...] + 1).astype(jnp.float32)
    lane = lax.broadcasted_iota(jnp.int32, (rows, columns), 1)
    pack = jnp.zeros((rows, columns), jnp.float32)
    for plane in range(PLANES):
        value = block[plane]
        if plane:
            value = pltpu.roll(value, span * plane, 1)
        place = (lane - (span * plane - STEPS)) & (columns - 1)
        pack = jnp.where(place < span, value, pack)
    packed[...] = pack

    load_away.wait()
    for index in range(half):
        bulk[index] = spectrum[other * half + index].reshape(4 * rows_all, columns).astype(jnp.bfloat16)
    for copy in inputs[2:4]:
        copy.wait()

    beside = lax.div(space + spaces - 1, spaces) + lax.div(2 * spaces - 2 - space, spaces)
    pl.semaphore_wait(barrier, count - 1 + count * beside)

    def halo_copy(side, step, at, slot):
        return pltpu.make_async_remote_copy(
            src_ref=packed, dst_ref=halo.at[side, slot],
            send_sem=halo_send.at[side], recv_sem=halo_recv.at[side],
            device_id=device(step, at), device_id_type=MESH,
        )

    def center_copy(step, slot):
        return pltpu.make_async_remote_copy(
            src_ref=block, dst_ref=center.at[slot],
            send_sem=center_send, recv_sem=center_recv,
            device_id=device(step, space), device_id_type=MESH,
        )

    def group_wait(buffer, semaphore):
        pltpu.make_async_copy(buffer, buffer, semaphore).wait()

    partner = {"role": other, "space": space, "freq": group}
    cells_copy = pltpu.make_async_remote_copy(
        src_ref=cells, dst_ref=cells_far, send_sem=small_send.at[0], recv_sem=small_recv.at[0],
        device_id=partner, device_id_type=MESH,
    )
    wavelets_copy = pltpu.make_async_remote_copy(
        src_ref=wavelets, dst_ref=wavelets_far, send_sem=small_send.at[1], recv_sem=small_recv.at[1],
        device_id=partner, device_id_type=MESH,
    )
    bulk_copy = pltpu.make_async_remote_copy(
        src_ref=bulk, dst_ref=bulk_far, send_sem=bulk_send, recv_sem=bulk_recv,
        device_id=partner, device_id_type=MESH,
    )

    @pl.when(has_high)
    def _():
        for step in range(count):
            halo_copy(0, step, space + 1, me).start()

    @pl.when(has_low)
    def _():
        for step in range(count):
            halo_copy(1, step, space - 1, me).start()

    for step in range(1, count):
        center_copy(step, me).start()
    cells_copy.start()
    wavelets_copy.start()

    bulk_copy.start()
    for copy in inputs[4:]:
        copy.wait()

    depth = 2 * STEPS * rows_all
    at_row = lax.broadcasted_iota(jnp.int32, (2 * rows_all, depth), 0)
    at_lane = lax.broadcasted_iota(jnp.int32, (2 * rows_all, depth), 1)
    step_of = (at_lane >> log2(rows_all)) & (STEPS - 1)
    turn = jnp.where(at_lane >= STEPS * rows_all, PERIOD // 4, 0)
    match = (at_lane & (rows_all - 1)) == (at_row & (rows_all - 1))
    for pair in range(local_freqs // 2):
        number = jnp.where(at_row < rows_all, freq_index[2 * pair], freq_index[2 * pair + 1])
        turns = (number * step_of + turn) & (PERIOD - 1)
        value = jnp.cos(turns.astype(jnp.float32) * (TWO_PI / PERIOD))
        table[pl.ds(pair * 2 * rows_all, 2 * rows_all), :] = jnp.where(match, value, 0.0).astype(jnp.bfloat16)

    def injection(which, cell_row, wavelet_rows):
        cell_at = jnp.broadcast_to(cell_row, (rows_all, nsrc)) >> log2(columns * spaces)
        row_at = lax.broadcasted_iota(jnp.int32, (rows_all, nsrc), 0)
        for tick in range(STEPS):
            amount = jnp.broadcast_to(wavelet_rows[tick:tick + 1, :], (rows_all, nsrc))
            inject_left[pl.ds(tick * rows_all, rows_all), :] = jnp.where(cell_at == row_at, amount, 0.0)
        column_at = lax.broadcasted_iota(jnp.int32, (wide, nsrc), 0)
        shift = jnp.where(column_at >= wide - STEPS, column_at - wide, column_at) + space * columns
        shift = jnp.where((column_at >= columns + STEPS) & (column_at < wide - STEPS), -1, shift)
        wanted = jnp.broadcast_to(cell_row, (wide, nsrc)) & (columns * spaces - 1)
        hit = (shift == wanted).astype(jnp.float32)
        inject[which] = lax.dot_general(
            inject_left[...], hit, (((1,), (1,)), ((), ())),
            precision=lax.Precision.HIGHEST, preferred_element_type=jnp.float32,
        )

    injection(0, cells[...], wavelets[0])

    cells_copy.wait_recv()
    wavelets_copy.wait_recv()
    injection(1, cells_far[...], wavelets_far[0])

    group_wait(center.at[pl.ds(0, count - 1)], center_recv)
    for plane in range(PLANES):
        center[me, plane] = block[plane]

    for which, owner in ((0, role), (1, other)):
        for part in range(groups):
            slot = owner * groups + part
            for plane in range(PLANES):
                planes[which, plane, pl.ds(part * rows, rows), :] = center[slot, plane]

    @pl.when(has_low)
    def _():
        group_wait(halo.at[0], halo_recv.at[0])

    @pl.when(has_high)
    def _():
        group_wait(halo.at[1], halo_recv.at[1])

    low_part = (lane & (span - 1)) < STEPS
    for which, owner in ((0, role), (1, other)):
        for part in range(groups):
            slot = owner * groups + part
            edges[which, pl.ds(part * rows, rows), :] = jnp.where(low_part, halo[1, slot], halo[0, slot])

    lane_all = lax.broadcasted_iota(jnp.int32, (rows_all, columns), 1)
    rim = (lane_all < STEPS) | (lane_all >= columns - STEPS)

    def whole(which, plane):
        outer = edges[which]
        if plane:
            outer = pltpu.roll(outer, columns - span * plane, 1)
        return jnp.concatenate([planes[which, plane], jnp.where(rim, outer, 0.0)], axis=1)

    ident = whole(0, PLANES - 1)
    props = [jnp.zeros_like(ident) for _ in range(3)]
    for block_id in range(nmat):
        same = ident == float(block_id + 1)
        props = [jnp.where(same, material[k, block_id], props[k]) for k in range(3)]
    buoyancy = COURANT * props[0]
    first = COURANT * props[1]
    second = COURANT * props[2]
    stiff = first + 2.0 * second

    row_id = lax.broadcasted_iota(jnp.int32, (rows_all, wide), 0)
    not_top = row_id > 0
    not_end = row_id < rows_all - 1

    def up(x):
        return jnp.where(not_end, pltpu.roll(x, rows_all - 1, 0), 0.0)

    def down(x):
        return jnp.where(not_top, pltpu.roll(x, 1, 0), 0.0)

    def right(x):
        return pltpu.roll(x, wide - 1, 1)

    def left(x):
        return pltpu.roll(x, 1, 1)

    state = [[whole(which, plane) for plane in range(5)] for which in range(2)]
    for tick in range(STEPS):
        at = pl.ds(tick * rows_all, rows_all)
        for which in range(2):
            vx, vz, xx, zz, xz = state[which]
            vx = vx + buoyancy * ((up(xx) - xx) + (xz - left(xz)))
            vz = vz + buoyancy * ((xz - down(xz)) + (right(zz) - zz))
            source = inject[which, at, :]
            ex = vx - down(vx)
            ez = vz - left(vz)
            xx = xx + (stiff * ex + first * ez) + source
            zz = zz + (first * ex + stiff * ez) + source
            xz = xz + second * ((right(vx) - vx) + (up(vz) - vz))
            state[which] = [vx, vz, xx, zz, xz]
            snaps[which, at, 0:columns] = vx[:, :columns]
            snaps[which, at, columns:wide] = vz[:, :columns]
    for plane in range(5):
        final[plane] = state[0][plane][:, :columns]
    for plane in range(5):
        fields_out[0, plane] = final[plane, pl.ds(group * rows, rows), :]

    def right_side(which):
        snap = snaps[which].astype(jnp.bfloat16)
        zero = jnp.zeros_like(snap)
        return jnp.concatenate(
            [jnp.concatenate([snap, zero], axis=1), jnp.concatenate([zero, snap], axis=1)], axis=0
        )

    def products(which_freqs, side):
        lines = pl.ds(pl.multiple_of(which_freqs * half * rows_all, 16), half * rows_all)
        return jnp.dot(table[lines, :], side, preferred_element_type=jnp.float32)

    def piece(value, index, part):
        return value[index * rows_all:(index + 1) * rows_all, part * columns:(part + 1) * columns]

    load_home.wait()
    side = right_side(0)
    near = products(role, side)
    far = products(role, right_side(1))
    bulk_copy.wait_recv()
    total = jnp.zeros((rows_all, columns), jnp.float32)
    for index in range(half):
        theirs = bulk_far[index].astype(jnp.float32)
        term = jnp.zeros((rows_all, columns), jnp.float32)
        for part in range(4):
            mine = spectrum[role * half + index, part] + piece(near, index, part)
            spectrum[role * half + index, part] = mine
            term = term + mine * (theirs[part * rows_all:(part + 1) * rows_all] + piece(far, index, part))
        total = total + freq_weight[role * half + index] * term
    total = total * (1.0 / (local_freqs * groups))
    each = rows_all // count
    for slot in range(count):
        sums[slot] = total[slot * each:(slot + 1) * each]

    def sums_copy(step, slot):
        return pltpu.make_async_remote_copy(
            src_ref=sums.at[peer(step)], dst_ref=sums_far.at[slot],
            send_sem=sums_send, recv_sem=sums_recv,
            device_id=device(step, space), device_id_type=MESH,
        )

    for step in range(1, count):
        sums_copy(step, me).start()
    rest = products(other, side)
    for index in range(half):
        for part in range(4):
            spectrum[other * half + index, part] = spectrum[other * half + index, part] + piece(rest, index, part)

    answer = sums[me]
    group_wait(sums.at[pl.ds(0, count - 1)], sums_recv)
    for step in range(1, count):
        answer = answer + sums_far[peer(step)]
    gradient[...] = answer

    @pl.when(has_high)
    def _():
        group_wait(halo.at[0], halo_send.at[0])

    @pl.when(has_low)
    def _():
        group_wait(halo.at[1], halo_send.at[1])

    group_wait(center.at[pl.ds(0, count - 1)], center_send)
    group_wait(sums.at[pl.ds(0, count - 1)], sums_send)
    cells_copy.wait_send()
    wavelets_copy.wait_send()
    bulk_copy.wait_send()


def deliver(fields, spectrum, gradient, fields_out, spectra_out, gradient_out, sem):
    each = spectrum.shape[0] // PIECES
    copies = [
        pltpu.make_async_copy(
            spectrum.at[pl.ds(piece * each, each)], spectra_out.at[0, pl.ds(piece * each, each)], sem.at[piece]
        )
        for piece in range(PIECES)
    ]
    copies.append(pltpu.make_async_copy(fields, fields_out, sem.at[PIECES]))
    copies.append(pltpu.make_async_copy(gradient, gradient_out, sem.at[PIECES + 1]))
    for copy in copies:
        copy.start()
    for copy in copies:
        copy.wait()


def local(fields, spectra, freq_index, freq_weight, material_ids, material, source_cells, wavelets):
    groups = lax.axis_size("freq")
    spaces = lax.axis_size("space")
    rows, columns = fields.shape[2:]
    local_freqs = freq_index.shape[0]
    rows_all = rows * groups
    count = 2 * groups
    half = local_freqs // 2
    nsrc = source_cells.shape[1]
    wide = 2 * columns
    sizes = (groups, spaces, local_freqs, rows, columns)
    f32 = jnp.float32
    vmem = pl.BlockSpec(memory_space=pltpu.VMEM)
    anywhere = pl.BlockSpec(memory_space=pl.ANY)
    dma = pltpu.SemaphoreType.DMA
    results = pl.pallas_call(
        functools.partial(kernel, sizes),
        out_shape=(
            pltpu.VMEM(fields.shape, f32),
            pltpu.VMEM(spectra.shape[1:], f32),
            pltpu.VMEM((rows_all // count, columns), f32),
        ),
        in_specs=[anywhere] * 8,
        out_specs=(vmem, vmem, vmem),
        scratch_shapes=[
            pltpu.VMEM((rows, columns), jnp.int32),
            pltpu.SMEM((local_freqs,), jnp.int32),
            pltpu.SMEM((local_freqs,), f32),
            pltpu.SMEM(material.shape, f32),
            pltpu.VMEM((1, nsrc), jnp.int32),
            pltpu.VMEM((1, STEPS, nsrc), f32),
            pltpu.VMEM((PLANES, rows, columns), f32),
            pltpu.VMEM((rows, columns), f32),
            pltpu.VMEM((count, PLANES, rows, columns), f32),
            pltpu.VMEM((2, count, rows, columns), f32),
            pltpu.VMEM((1, nsrc), jnp.int32),
            pltpu.VMEM((1, STEPS, nsrc), f32),
            pltpu.VMEM((2, PLANES, rows_all, columns), f32),
            pltpu.VMEM((2, rows_all, columns), f32),
            pltpu.VMEM((STEPS * rows_all, nsrc), f32),
            pltpu.VMEM((2, STEPS * rows_all, wide), f32),
            pltpu.VMEM((local_freqs * rows_all, 2 * STEPS * rows_all), jnp.bfloat16),
            pltpu.VMEM((2, STEPS * rows_all, wide), f32),
            pltpu.VMEM((half, 4 * rows_all, columns), jnp.bfloat16),
            pltpu.VMEM((half, 4 * rows_all, columns), jnp.bfloat16),
            pltpu.VMEM((5, rows_all, columns), f32),
            pltpu.VMEM((count, rows_all // count, columns), f32),
            pltpu.VMEM((count, rows_all // count, columns), f32),
            dma, dma, dma((2,)), dma((2,)), dma((2,)), dma((2,)),
            dma, dma, dma, dma, dma((2,)), dma((7,)),
        ],
        compiler_params=pltpu.CompilerParams(collective_id=0, has_side_effects=True),
    )(fields, material_ids, freq_index, freq_weight, material, source_cells, wavelets, spectra)
    return tuple(pl.pallas_call(
        deliver,
        out_shape=(
            jax.ShapeDtypeStruct(fields.shape, f32),
            jax.ShapeDtypeStruct(spectra.shape, f32),
            jax.ShapeDtypeStruct((rows_all // count, columns), f32),
        ),
        in_specs=[vmem, vmem, vmem],
        out_specs=(anywhere, anywhere, anywhere),
        scratch_shapes=[dma((PIECES + 2,))],
    )(*[pltpu.with_memory_space_constraint(x, pltpu.VMEM) for x in results]))


def solution(mesh):
    return jax.shard_map(
        local,
        mesh=mesh,
        in_specs=(
            P("role", None, "freq", "space"),
            P("role", "freq", None, None, "space"),
            P("freq"),
            P("freq"),
            P("freq", "space"),
            P(),
            P("role", None),
            P("role", None, None),
        ),
        out_specs=(
            P("role", None, "freq", "space"),
            P("role", "freq", None, None, "space"),
            P(("role", "freq"), "space"),
        ),
        check_vma=False,
    )
```

```python
import functools
import math

import jax
import jax.numpy as jnp
from jax import lax
from jax.experimental import pallas as pl
from jax.experimental.pallas import tpu as pltpu
from jax.sharding import PartitionSpec as P

STEPS = 8
PERIOD = 64
COURANT = 0.18
TWO_PI = 6.283185307179586
PLANES = 6
PIECES = 1
MESH = pl.DeviceIdType.MESH


def log2(n):
    bits = n.bit_length() - 1
    assert n == 1 << bits
    return bits


def kernel(
    sizes,
    fields_in, ids_in, freq_index_in, freq_weight_in, material_in, cells_in, wavelets_in, spectra,
    fields_out, spectrum, gradient,
    ids, freq_index, freq_weight, material, cells, wavelets,
    block, packed, center, halo, cells_far, wavelets_far, planes,
    inject_left, inject, table, snaps, bulk, bulk_far, final, sums, sums_far,
    center_send, center_recv, halo_send, halo_recv, small_send, small_recv,
    bulk_send, bulk_recv, sums_send, sums_recv, load_sem, input_sem,
):
    groups, spaces, local_freqs, rows, columns = sizes
    count = 2 * groups
    rows_all = rows * groups
    span = 2 * STEPS
    wide = 2 * columns
    half = local_freqs // 2
    nmat = material.shape[1]
    nsrc = cells.shape[1]
    role = lax.axis_index("role")
    space = lax.axis_index("space")
    group = lax.axis_index("freq")
    other = 1 - role
    me = role * groups + group

    places = []
    for flip in (role, other):
        for step in range(groups):
            places.append((flip, lax.rem(group + step, groups)))
    slots = [flip * groups + at for flip, at in places]

    def device(step, at):
        return {"role": places[step][0], "space": at, "freq": places[step][1]}

    def peer(step):
        return slots[step]

    away = pl.ds(other * half, half)
    home = pl.ds(role * half, half)
    load_away = pltpu.make_async_copy(spectra.at[0, away], spectrum.at[away], load_sem.at[0])
    load_home = pltpu.make_async_copy(spectra.at[0, home], spectrum.at[home], load_sem.at[1])
    inputs = [
        pltpu.make_async_copy(source, target, input_sem.at[index])
        for index, (source, target) in enumerate((
            (fields_in.at[0], block.at[pl.ds(0, PLANES - 1)]), (ids_in, ids), (cells_in, cells),
            (wavelets_in, wavelets), (freq_index_in, freq_index), (material_in, material),
            (freq_weight_in, freq_weight),
        ))
    ]

    has_low = space > 0
    has_high = space < spaces - 1

    for copy in inputs:
        copy.start()

    halo[...] = jnp.zeros_like(halo)

    barrier = pltpu.get_barrier_semaphore()

    @pl.when(has_low)
    def _():
        pl.semaphore_signal(barrier, inc=1, device_id=device(0, space - 1), device_id_type=MESH)

    @pl.when(has_high)
    def _():
        pl.semaphore_signal(barrier, inc=1, device_id=device(0, space + 1), device_id_type=MESH)

    for step in range(1, count):
        pl.semaphore_signal(barrier, inc=1, device_id=device(step, space), device_id_type=MESH)

    load_away.start()
    load_home.start()
    for copy in inputs[:2]:
        copy.wait()

    block[PLANES - 1] = (ids[...] + 1).astype(jnp.float32)

    load_away.wait()
    for index in range(half):
        bulk[index] = spectrum[other * half + index].reshape(4 * rows_all, columns).astype(jnp.bfloat16)
    for copy in inputs[2:4]:
        copy.wait()

    beside = lax.div(space + spaces - 1, spaces) + lax.div(2 * spaces - 2 - space, spaces)
    pl.semaphore_wait(barrier, count - 1 + beside)

    def halo_copy(side, at):
        return pltpu.make_async_remote_copy(
            src_ref=packed, dst_ref=halo.at[side], send_sem=halo_send.at[side], recv_sem=halo_recv.at[side],
            device_id=device(0, at), device_id_type=MESH,
        )

    def center_copy(step, slot):
        return pltpu.make_async_remote_copy(
            src_ref=block, dst_ref=center.at[slot],
            send_sem=center_send, recv_sem=center_recv,
            device_id=device(step, space), device_id_type=MESH,
        )

    def group_wait(buffer, semaphore):
        pltpu.make_async_copy(buffer, buffer, semaphore).wait()

    partner = {"role": other, "space": space, "freq": group}
    cells_copy = pltpu.make_async_remote_copy(
        src_ref=cells, dst_ref=cells_far, send_sem=small_send.at[0], recv_sem=small_recv.at[0],
        device_id=partner, device_id_type=MESH,
    )
    wavelets_copy = pltpu.make_async_remote_copy(
        src_ref=wavelets, dst_ref=wavelets_far, send_sem=small_send.at[1], recv_sem=small_recv.at[1],
        device_id=partner, device_id_type=MESH,
    )
    bulk_copy = pltpu.make_async_remote_copy(
        src_ref=bulk, dst_ref=bulk_far, send_sem=bulk_send, recv_sem=bulk_recv,
        device_id=partner, device_id_type=MESH,
    )

    for step in range(1, count):
        center_copy(step, me).start()
    cells_copy.start()
    wavelets_copy.start()

    bulk_copy.start()
    for copy in inputs[4:]:
        copy.wait()

    depth = 2 * STEPS * rows_all
    at_row = lax.broadcasted_iota(jnp.int32, (2 * rows_all, depth), 0)
    at_lane = lax.broadcasted_iota(jnp.int32, (2 * rows_all, depth), 1)
    step_of = (at_lane >> log2(rows_all)) & (STEPS - 1)
    turn = jnp.where(at_lane >= STEPS * rows_all, PERIOD // 4, 0)
    match = (at_lane & (rows_all - 1)) == (at_row & (rows_all - 1))
    for pair in range(local_freqs // 2):
        number = jnp.where(at_row < rows_all, freq_index[2 * pair], freq_index[2 * pair + 1])
        turns = (number * step_of + turn) & (PERIOD - 1)
        value = jnp.cos(turns.astype(jnp.float32) * (TWO_PI / PERIOD))
        table[pl.ds(pair * 2 * rows_all, 2 * rows_all), :] = jnp.where(match, value, 0.0).astype(jnp.bfloat16)

    def injection(which, cell_row, wavelet_rows):
        cell_at = jnp.broadcast_to(cell_row, (rows_all, nsrc)) >> log2(columns * spaces)
        row_at = lax.broadcasted_iota(jnp.int32, (rows_all, nsrc), 0)
        for tick in range(STEPS):
            amount = jnp.broadcast_to(wavelet_rows[tick:tick + 1, :], (rows_all, nsrc))
            inject_left[pl.ds(tick * rows_all, rows_all), :] = jnp.where(cell_at == row_at, amount, 0.0)
        column_at = lax.broadcasted_iota(jnp.int32, (wide, nsrc), 0)
        shift = jnp.where(column_at >= wide - STEPS, column_at - wide, column_at) + space * columns
        shift = jnp.where((column_at >= columns + STEPS) & (column_at < wide - STEPS), -1, shift)
        wanted = jnp.broadcast_to(cell_row, (wide, nsrc)) & (columns * spaces - 1)
        hit = (shift == wanted).astype(jnp.float32)
        inject[which] = lax.dot_general(
            inject_left[...], hit, (((1,), (1,)), ((), ())),
            precision=lax.Precision.HIGHEST, preferred_element_type=jnp.float32,
        )

    injection(0, cells[...], wavelets[0])

    group_wait(center.at[pl.ds(0, count - 1)], center_recv)
    for plane in range(PLANES):
        center[me, plane] = block[plane]

    for which, owner in ((0, role), (1, other)):
        for part in range(groups):
            slot = owner * groups + part
            for plane in range(PLANES):
                planes[which, plane, pl.ds(part * rows, rows), :] = center[slot, plane]

    lane_all = lax.broadcasted_iota(jnp.int32, (rows_all, columns), 1)
    for which in range(2):
        pack = jnp.zeros((rows_all, columns), jnp.float32)
        for plane in range(PLANES):
            value = planes[which, plane]
            if plane:
                value = pltpu.roll(value, span * plane, 1)
            place = (lane_all - (span * plane - STEPS)) & (columns - 1)
            pack = jnp.where(place < span, value, pack)
        packed[which] = pack

    @pl.when(has_high)
    def _():
        halo_copy(0, space + 1).start()

    @pl.when(has_low)
    def _():
        halo_copy(1, space - 1).start()

    rim = (lane_all < STEPS) | (lane_all >= columns - STEPS)

    low_part = (lane_all & (span - 1)) < STEPS

    def outside(which):
        return jnp.where(low_part, halo[1, which], halo[0, which])

    def whole(which, plane):
        outer = outer_of[which]
        if plane:
            outer = pltpu.roll(outer, columns - span * plane, 1)
        return jnp.concatenate([planes[which, plane], jnp.where(rim, outer, 0.0)], axis=1)

    cells_copy.wait_recv()
    wavelets_copy.wait_recv()
    injection(1, cells_far[...], wavelets_far[0])

    @pl.when(has_low)
    def _():
        group_wait(halo.at[0], halo_recv.at[0])

    @pl.when(has_high)
    def _():
        group_wait(halo.at[1], halo_recv.at[1])

    outer_of = [outside(0), outside(1)]
    ident = whole(0, PLANES - 1)
    props = [jnp.zeros_like(ident) for _ in range(3)]
    for block_id in range(nmat):
        same = ident == float(block_id + 1)
        props = [jnp.where(same, material[k, block_id], props[k]) for k in range(3)]
    buoyancy = COURANT * props[0]
    first = COURANT * props[1]
    second = COURANT * props[2]
    stiff = first + 2.0 * second

    row_id = lax.broadcasted_iota(jnp.int32, (rows_all, wide), 0)
    not_top = row_id > 0
    not_end = row_id < rows_all - 1

    def up(x):
        return jnp.where(not_end, pltpu.roll(x, rows_all - 1, 0), 0.0)

    def down(x):
        return jnp.where(not_top, pltpu.roll(x, 1, 0), 0.0)

    def right(x):
        return pltpu.roll(x, wide - 1, 1)

    def left(x):
        return pltpu.roll(x, 1, 1)

    state = [[whole(which, plane) for plane in range(5)] for which in range(2)]
    for tick in range(STEPS):
        at = pl.ds(tick * rows_all, rows_all)
        for which in range(2):
            vx, vz, xx, zz, xz = state[which]
            vx = vx + buoyancy * ((up(xx) - xx) + (xz - left(xz)))
            vz = vz + buoyancy * ((xz - down(xz)) + (right(zz) - zz))
            source = inject[which, at, :]
            ex = vx - down(vx)
            ez = vz - left(vz)
            xx = xx + (stiff * ex + first * ez) + source
            zz = zz + (first * ex + stiff * ez) + source
            xz = xz + second * ((right(vx) - vx) + (up(vz) - vz))
            state[which] = [vx, vz, xx, zz, xz]
            snaps[which, at, 0:columns] = vx[:, :columns]
            snaps[which, at, columns:wide] = vz[:, :columns]
    for plane in range(5):
        final[plane] = state[0][plane][:, :columns]
    for plane in range(5):
        fields_out[0, plane] = final[plane, pl.ds(group * rows, rows), :]

    def right_side(which):
        snap = snaps[which].astype(jnp.bfloat16)
        zero = jnp.zeros_like(snap)
        return jnp.concatenate(
            [jnp.concatenate([snap, zero], axis=1), jnp.concatenate([zero, snap], axis=1)], axis=0
        )

    def products(which_freqs, side):
        lines = pl.ds(pl.multiple_of(which_freqs * half * rows_all, 16), half * rows_all)
        return jnp.dot(table[lines, :], side, preferred_element_type=jnp.float32)

    def piece(value, index, part):
        return value[index * rows_all:(index + 1) * rows_all, part * columns:(part + 1) * columns]

    load_home.wait()
    side = right_side(0)
    near = products(role, side)
    far = products(role, right_side(1))
    bulk_copy.wait_recv()
    total = jnp.zeros((rows_all, columns), jnp.float32)
    for index in range(half):
        theirs = bulk_far[index].astype(jnp.float32)
        term = jnp.zeros((rows_all, columns), jnp.float32)
        for part in range(4):
            mine = spectrum[role * half + index, part] + piece(near, index, part)
            spectrum[role * half + index, part] = mine
            term = term + mine * (theirs[part * rows_all:(part + 1) * rows_all] + piece(far, index, part))
        total = total + freq_weight[role * half + index] * term
    total = total * (1.0 / (local_freqs * groups))
    each = rows_all // count
    for slot in range(count):
        sums[slot] = total[slot * each:(slot + 1) * each]

    def sums_copy(step, slot):
        return pltpu.make_async_remote_copy(
            src_ref=sums.at[peer(step)], dst_ref=sums_far.at[slot],
            send_sem=sums_send, recv_sem=sums_recv,
            device_id=device(step, space), device_id_type=MESH,
        )

    for step in range(1, count):
        sums_copy(step, me).start()
    rest = products(other, side)
    for index in range(half):
        for part in range(4):
            spectrum[other * half + index, part] = spectrum[other * half + index, part] + piece(rest, index, part)

    answer = sums[me]
    group_wait(sums.at[pl.ds(0, count - 1)], sums_recv)
    for step in range(1, count):
        answer = answer + sums_far[peer(step)]
    gradient[...] = answer

    @pl.when(has_high)
    def _():
        group_wait(halo.at[0], halo_send.at[0])

    @pl.when(has_low)
    def _():
        group_wait(halo.at[1], halo_send.at[1])

    group_wait(center.at[pl.ds(0, count - 1)], center_send)
    group_wait(sums.at[pl.ds(0, count - 1)], sums_send)
    cells_copy.wait_send()
    wavelets_copy.wait_send()
    bulk_copy.wait_send()


def deliver(fields, spectrum, gradient, fields_out, spectra_out, gradient_out, sem):
    each = spectrum.shape[0] // PIECES
    copies = [
        pltpu.make_async_copy(
            spectrum.at[pl.ds(piece * each, each)], spectra_out.at[0, pl.ds(piece * each, each)], sem.at[piece]
        )
        for piece in range(PIECES)
    ]
    copies.append(pltpu.make_async_copy(fields, fields_out, sem.at[PIECES]))
    copies.append(pltpu.make_async_copy(gradient, gradient_out, sem.at[PIECES + 1]))
    for copy in copies:
        copy.start()
    for copy in copies:
        copy.wait()


def local(fields, spectra, freq_index, freq_weight, material_ids, material, source_cells, wavelets):
    groups = lax.axis_size("freq")
    spaces = lax.axis_size("space")
    rows, columns = fields.shape[2:]
    local_freqs = freq_index.shape[0]
    rows_all = rows * groups
    count = 2 * groups
    half = local_freqs // 2
    nsrc = source_cells.shape[1]
    wide = 2 * columns
    sizes = (groups, spaces, local_freqs, rows, columns)
    f32 = jnp.float32
    vmem = pl.BlockSpec(memory_space=pltpu.VMEM)
    anywhere = pl.BlockSpec(memory_space=pl.ANY)
    dma = pltpu.SemaphoreType.DMA
    results = pl.pallas_call(
        functools.partial(kernel, sizes),
        out_shape=(
            pltpu.VMEM(fields.shape, f32),
            pltpu.VMEM(spectra.shape[1:], f32),
            pltpu.VMEM((rows_all // count, columns), f32),
        ),
        in_specs=[anywhere] * 8,
        out_specs=(vmem, vmem, vmem),
        scratch_shapes=[
            pltpu.VMEM((rows, columns), jnp.int32),
            pltpu.SMEM((local_freqs,), jnp.int32),
            pltpu.SMEM((local_freqs,), f32),
            pltpu.SMEM(material.shape, f32),
            pltpu.VMEM((1, nsrc), jnp.int32),
            pltpu.VMEM((1, STEPS, nsrc), f32),
            pltpu.VMEM((PLANES, rows, columns), f32),
            pltpu.VMEM((2, rows_all, columns), f32),
            pltpu.VMEM((count, PLANES, rows, columns), f32),
            pltpu.VMEM((2, 2, rows_all, columns), f32),
            pltpu.VMEM((1, nsrc), jnp.int32),
            pltpu.VMEM((1, STEPS, nsrc), f32),
            pltpu.VMEM((2, PLANES, rows_all, columns), f32),
            pltpu.VMEM((STEPS * rows_all, nsrc), f32),
            pltpu.VMEM((2, STEPS * rows_all, wide), f32),
            pltpu.VMEM((local_freqs * rows_all, 2 * STEPS * rows_all), jnp.bfloat16),
            pltpu.VMEM((2, STEPS * rows_all, wide), f32),
            pltpu.VMEM((half, 4 * rows_all, columns), jnp.bfloat16),
            pltpu.VMEM((half, 4 * rows_all, columns), jnp.bfloat16),
            pltpu.VMEM((5, rows_all, columns), f32),
            pltpu.VMEM((count, rows_all // count, columns), f32),
            pltpu.VMEM((count, rows_all // count, columns), f32),
            dma, dma, dma((2,)), dma((2,)), dma((2,)), dma((2,)),
            dma, dma, dma, dma, dma((2,)), dma((7,)),
        ],
        compiler_params=pltpu.CompilerParams(collective_id=0, has_side_effects=True),
    )(fields, material_ids, freq_index, freq_weight, material, source_cells, wavelets, spectra)
    return tuple(pl.pallas_call(
        deliver,
        out_shape=(
            jax.ShapeDtypeStruct(fields.shape, f32),
            jax.ShapeDtypeStruct(spectra.shape, f32),
            jax.ShapeDtypeStruct((rows_all // count, columns), f32),
        ),
        in_specs=[vmem, vmem, vmem],
        out_specs=(anywhere, anywhere, anywhere),
        scratch_shapes=[dma((PIECES + 2,))],
    )(*[pltpu.with_memory_space_constraint(x, pltpu.VMEM) for x in results]))


def solution(mesh):
    return jax.shard_map(
        local,
        mesh=mesh,
        in_specs=(
            P("role", None, "freq", "space"),
            P("role", "freq", None, None, "space"),
            P("freq"),
            P("freq"),
            P("freq", "space"),
            P(),
            P("role", None),
            P("role", None, None),
        ),
        out_specs=(
            P("role", None, "freq", "space"),
            P("role", "freq", None, None, "space"),
            P(("role", "freq"), "space"),
        ),
        check_vma=False,
    )
```

```python
import functools
import math

import jax
import jax.numpy as jnp
from jax import lax
from jax.experimental import pallas as pl
from jax.experimental.pallas import tpu as pltpu
from jax.sharding import PartitionSpec as P

STEPS = 8
PERIOD = 64
COURANT = 0.18
TWO_PI = 6.283185307179586
PLANES = 6
PIECES = 1
MESH = pl.DeviceIdType.MESH


def log2(n):
    bits = n.bit_length() - 1
    assert n == 1 << bits
    return bits


def kernel(
    sizes,
    fields_in, ids_in, freq_index_in, freq_weight_in, material_in, cells_in, wavelets_in, spectra,
    fields_out, spectrum, gradient,
    ids, freq_index, freq_weight, material, cells, wavelets,
    block, packed, center, halo, cells_far, wavelets_far, planes, edges,
    inject_left, inject, table, snaps, bulk, bulk_far, final, sums, sums_far,
    center_send, center_recv, halo_send, halo_recv, small_send, small_recv,
    bulk_send, bulk_recv, sums_send, sums_recv, load_sem, input_sem,
):
    groups, spaces, local_freqs, rows, columns = sizes
    count = 2 * groups
    rows_all = rows * groups
    span = 2 * STEPS
    wide = 2 * columns
    half = local_freqs // 2
    nmat = material.shape[1]
    nsrc = cells.shape[1]
    role = lax.axis_index("role")
    space = lax.axis_index("space")
    group = lax.axis_index("freq")
    other = 1 - role
    me = role * groups + group

    places = []
    for flip in (role, other):
        for step in range(groups):
            places.append((flip, lax.rem(group + step, groups)))
    slots = [flip * groups + at for flip, at in places]

    def device(step, at):
        return {"role": places[step][0], "space": at, "freq": places[step][1]}

    def peer(step):
        return slots[step]

    away = pl.ds(other * half, half)
    home = pl.ds(role * half, half)
    load_away = pltpu.make_async_copy(spectra.at[0, away], spectrum.at[away], load_sem.at[0])
    load_home = pltpu.make_async_copy(spectra.at[0, home], spectrum.at[home], load_sem.at[1])
    inputs = [
        pltpu.make_async_copy(source, target, input_sem.at[index])
        for index, (source, target) in enumerate((
            (fields_in.at[0], block.at[pl.ds(0, PLANES - 1)]), (ids_in, ids), (cells_in, cells),
            (wavelets_in, wavelets), (freq_index_in, freq_index), (material_in, material),
            (freq_weight_in, freq_weight),
        ))
    ]

    has_low = space > 0
    has_high = space < spaces - 1

    for copy in inputs:
        copy.start()

    halo[...] = jnp.zeros_like(halo)

    barrier = pltpu.get_barrier_semaphore()

    @pl.when(has_low)
    def _():
        for step in range(count):
            pl.semaphore_signal(barrier, inc=1, device_id=device(step, space - 1), device_id_type=MESH)

    @pl.when(has_high)
    def _():
        for step in range(count):
            pl.semaphore_signal(barrier, inc=1, device_id=device(step, space + 1), device_id_type=MESH)

    for step in range(1, count):
        pl.semaphore_signal(barrier, inc=1, device_id=device(step, space), device_id_type=MESH)

    load_away.start()
    load_home.start()
    for copy in inputs[:2]:
        copy.wait()

    block[PLANES - 1] = (ids[...] + 1).astype(jnp.float32)
    lane = lax.broadcasted_iota(jnp.int32, (rows, columns), 1)
    pack = jnp.zeros((rows, columns), jnp.float32)
    for plane in range(PLANES):
        value = block[plane]
        if plane:
            value = pltpu.roll(value, span * plane, 1)
        place = (lane - (span * plane - STEPS)) & (columns - 1)
        pack = jnp.where(place < span, value, pack)
    packed[...] = pack

    for copy in inputs[2:4]:
        copy.wait()

    beside = lax.div(space + spaces - 1, spaces) + lax.div(2 * spaces - 2 - space, spaces)
    pl.semaphore_wait(barrier, count - 1 + count * beside)

    def halo_copy(side, step, at, slot):
        return pltpu.make_async_remote_copy(
            src_ref=packed, dst_ref=halo.at[side, slot],
            send_sem=halo_send.at[side], recv_sem=halo_recv.at[side],
            device_id=device(step, at), device_id_type=MESH,
        )

    def center_copy(step, slot):
        return pltpu.make_async_remote_copy(
            src_ref=block, dst_ref=center.at[slot],
            send_sem=center_send, recv_sem=center_recv,
            device_id=device(step, space), device_id_type=MESH,
        )

    def group_wait(buffer, semaphore):
        pltpu.make_async_copy(buffer, buffer, semaphore).wait()

    partner = {"role": other, "space": space, "freq": group}
    cells_copy = pltpu.make_async_remote_copy(
        src_ref=cells, dst_ref=cells_far, send_sem=small_send.at[0], recv_sem=small_recv.at[0],
        device_id=partner, device_id_type=MESH,
    )
    wavelets_copy = pltpu.make_async_remote_copy(
        src_ref=wavelets, dst_ref=wavelets_far, send_sem=small_send.at[1], recv_sem=small_recv.at[1],
        device_id=partner, device_id_type=MESH,
    )
    bulk_copy = pltpu.make_async_remote_copy(
        src_ref=bulk, dst_ref=bulk_far, send_sem=bulk_send, recv_sem=bulk_recv,
        device_id=partner, device_id_type=MESH,
    )

    @pl.when(has_high)
    def _():
        for step in range(count):
            halo_copy(0, step, space + 1, me).start()

    @pl.when(has_low)
    def _():
        for step in range(count):
            halo_copy(1, step, space - 1, me).start()

    for step in range(1, count):
        center_copy(step, me).start()
    cells_copy.start()
    wavelets_copy.start()

    load_away.wait()
    for index in range(half):
        bulk[index] = spectrum[other * half + index].reshape(4 * rows_all, columns).astype(jnp.bfloat16)
    bulk_copy.start()
    for copy in inputs[4:]:
        copy.wait()

    depth = 2 * STEPS * rows_all
    at_row = lax.broadcasted_iota(jnp.int32, (2 * rows_all, depth), 0)
    at_lane = lax.broadcasted_iota(jnp.int32, (2 * rows_all, depth), 1)
    step_of = (at_lane >> log2(rows_all)) & (STEPS - 1)
    turn = jnp.where(at_lane >= STEPS * rows_all, PERIOD // 4, 0)
    match = (at_lane & (rows_all - 1)) == (at_row & (rows_all - 1))
    for pair in range(local_freqs // 2):
        number = jnp.where(at_row < rows_all, freq_index[2 * pair], freq_index[2 * pair + 1])
        turns = (number * step_of + turn) & (PERIOD - 1)
        value = jnp.cos(turns.astype(jnp.float32) * (TWO_PI / PERIOD))
        table[pl.ds(pair * 2 * rows_all, 2 * rows_all), :] = jnp.where(match, value, 0.0).astype(jnp.bfloat16)

    def injection(which, cell_row, wavelet_rows):
        cell_at = jnp.broadcast_to(cell_row, (rows_all, nsrc)) >> log2(columns * spaces)
        row_at = lax.broadcasted_iota(jnp.int32, (rows_all, nsrc), 0)
        for tick in range(STEPS):
            amount = jnp.broadcast_to(wavelet_rows[tick:tick + 1, :], (rows_all, nsrc))
            inject_left[pl.ds(tick * rows_all, rows_all), :] = jnp.where(cell_at == row_at, amount, 0.0)
        column_at = lax.broadcasted_iota(jnp.int32, (wide, nsrc), 0)
        shift = jnp.where(column_at >= wide - STEPS, column_at - wide, column_at) + space * columns
        shift = jnp.where((column_at >= columns + STEPS) & (column_at < wide - STEPS), -1, shift)
        wanted = jnp.broadcast_to(cell_row, (wide, nsrc)) & (columns * spaces - 1)
        hit = (shift == wanted).astype(jnp.float32)
        inject[which] = lax.dot_general(
            inject_left[...], hit, (((1,), (1,)), ((), ())),
            precision=lax.Precision.HIGHEST, preferred_element_type=jnp.float32,
        )

    injection(0, cells[...], wavelets[0])

    cells_copy.wait_recv()
    wavelets_copy.wait_recv()
    injection(1, cells_far[...], wavelets_far[0])

    group_wait(center.at[pl.ds(0, count - 1)], center_recv)
    for plane in range(PLANES):
        center[me, plane] = block[plane]

    for which, owner in ((0, role), (1, other)):
        for part in range(groups):
            slot = owner * groups + part
            for plane in range(PLANES):
                planes[which, plane, pl.ds(part * rows, rows), :] = center[slot, plane]

    @pl.when(has_low)
    def _():
        group_wait(halo.at[0], halo_recv.at[0])

    @pl.when(has_high)
    def _():
        group_wait(halo.at[1], halo_recv.at[1])

    low_part = (lane & (span - 1)) < STEPS
    for which, owner in ((0, role), (1, other)):
        for part in range(groups):
            slot = owner * groups + part
            edges[which, pl.ds(part * rows, rows), :] = jnp.where(low_part, halo[1, slot], halo[0, slot])

    lane_all = lax.broadcasted_iota(jnp.int32, (rows_all, columns), 1)
    rim = (lane_all < STEPS) | (lane_all >= columns - STEPS)

    def whole(which, plane):
        outer = edges[which]
        if plane:
            outer = pltpu.roll(outer, columns - span * plane, 1)
        return jnp.concatenate([planes[which, plane], jnp.where(rim, outer, 0.0)], axis=1)

    ident = whole(0, PLANES - 1)
    props = [jnp.zeros_like(ident) for _ in range(3)]
    for block_id in range(nmat):
        same = ident == float(block_id + 1)
        props = [jnp.where(same, material[k, block_id], props[k]) for k in range(3)]
    buoyancy = COURANT * props[0]
    first = COURANT * props[1]
    second = COURANT * props[2]
    stiff = first + 2.0 * second

    row_id = lax.broadcasted_iota(jnp.int32, (rows_all, wide), 0)
    not_top = row_id > 0
    not_end = row_id < rows_all - 1

    def up(x):
        return jnp.where(not_end, pltpu.roll(x, rows_all - 1, 0), 0.0)

    def down(x):
        return jnp.where(not_top, pltpu.roll(x, 1, 0), 0.0)

    def right(x):
        return pltpu.roll(x, wide - 1, 1)

    def left(x):
        return pltpu.roll(x, 1, 1)

    state = [[whole(which, plane) for plane in range(5)] for which in range(2)]
    for tick in range(STEPS):
        at = pl.ds(tick * rows_all, rows_all)
        for which in range(2):
            vx, vz, xx, zz, xz = state[which]
            vx = vx + buoyancy * ((up(xx) - xx) + (xz - left(xz)))
            vz = vz + buoyancy * ((xz - down(xz)) + (right(zz) - zz))
            source = inject[which, at, :]
            ex = vx - down(vx)
            ez = vz - left(vz)
            xx = xx + (stiff * ex + first * ez) + source
            zz = zz + (first * ex + stiff * ez) + source
            xz = xz + second * ((right(vx) - vx) + (up(vz) - vz))
            state[which] = [vx, vz, xx, zz, xz]
            snaps[which, at, 0:columns] = vx[:, :columns]
            snaps[which, at, columns:wide] = vz[:, :columns]
    for plane in range(5):
        final[plane] = state[0][plane][:, :columns]
    for plane in range(5):
        fields_out[0, plane] = final[plane, pl.ds(group * rows, rows), :]

    def right_side(which):
        snap = snaps[which].astype(jnp.bfloat16)
        zero = jnp.zeros_like(snap)
        return jnp.concatenate(
            [jnp.concatenate([snap, zero], axis=1), jnp.concatenate([zero, snap], axis=1)], axis=0
        )

    def products(which_freqs, side):
        lines = pl.ds(pl.multiple_of(which_freqs * half * rows_all, 16), half * rows_all)
        return jnp.dot(table[lines, :], side, preferred_element_type=jnp.float32)

    def piece(value, index, part):
        return value[index * rows_all:(index + 1) * rows_all, part * columns:(part + 1) * columns]

    load_home.wait()
    side = right_side(0)
    near = products(role, side)
    far = products(role, right_side(1))
    bulk_copy.wait_recv()
    total = jnp.zeros((rows_all, columns), jnp.float32)
    for index in range(half):
        theirs = bulk_far[index].astype(jnp.float32)
        term = jnp.zeros((rows_all, columns), jnp.float32)
        for part in range(4):
            mine = spectrum[role * half + index, part] + piece(near, index, part)
            spectrum[role * half + index, part] = mine
            term = term + mine * (theirs[part * rows_all:(part + 1) * rows_all] + piece(far, index, part))
        total = total + freq_weight[role * half + index] * term
    total = total * (1.0 / (local_freqs * groups))
    each = rows_all // count
    for slot in range(count):
        sums[slot] = total[slot * each:(slot + 1) * each]

    def sums_copy(step, slot):
        return pltpu.make_async_remote_copy(
            src_ref=sums.at[peer(step)], dst_ref=sums_far.at[slot],
            send_sem=sums_send, recv_sem=sums_recv,
            device_id=device(step, space), device_id_type=MESH,
        )

    for step in range(1, count):
        sums_copy(step, me).start()
    rest = products(other, side)
    for index in range(half):
        for part in range(4):
            spectrum[other * half + index, part] = spectrum[other * half + index, part] + piece(rest, index, part)

    answer = sums[me]
    group_wait(sums.at[pl.ds(0, count - 1)], sums_recv)
    for step in range(1, count):
        answer = answer + sums_far[peer(step)]
    gradient[...] = answer

    @pl.when(has_high)
    def _():
        group_wait(halo.at[0], halo_send.at[0])

    @pl.when(has_low)
    def _():
        group_wait(halo.at[1], halo_send.at[1])

    group_wait(center.at[pl.ds(0, count - 1)], center_send)
    group_wait(sums.at[pl.ds(0, count - 1)], sums_send)
    cells_copy.wait_send()
    wavelets_copy.wait_send()
    bulk_copy.wait_send()


def deliver(fields, spectrum, gradient, fields_out, spectra_out, gradient_out, sem):
    each = spectrum.shape[0] // PIECES
    copies = [
        pltpu.make_async_copy(
            spectrum.at[pl.ds(piece * each, each)], spectra_out.at[0, pl.ds(piece * each, each)], sem.at[piece]
        )
        for piece in range(PIECES)
    ]
    copies.append(pltpu.make_async_copy(fields, fields_out, sem.at[PIECES]))
    copies.append(pltpu.make_async_copy(gradient, gradient_out, sem.at[PIECES + 1]))
    for copy in copies:
        copy.start()
    for copy in copies:
        copy.wait()


def local(fields, spectra, freq_index, freq_weight, material_ids, material, source_cells, wavelets):
    groups = lax.axis_size("freq")
    spaces = lax.axis_size("space")
    rows, columns = fields.shape[2:]
    local_freqs = freq_index.shape[0]
    rows_all = rows * groups
    count = 2 * groups
    half = local_freqs // 2
    nsrc = source_cells.shape[1]
    wide = 2 * columns
    sizes = (groups, spaces, local_freqs, rows, columns)
    f32 = jnp.float32
    vmem = pl.BlockSpec(memory_space=pltpu.VMEM)
    anywhere = pl.BlockSpec(memory_space=pl.ANY)
    dma = pltpu.SemaphoreType.DMA
    results = pl.pallas_call(
        functools.partial(kernel, sizes),
        out_shape=(
            pltpu.VMEM(fields.shape, f32),
            pltpu.VMEM(spectra.shape[1:], f32),
            pltpu.VMEM((rows_all // count, columns), f32),
        ),
        in_specs=[anywhere] * 8,
        out_specs=(vmem, vmem, vmem),
        scratch_shapes=[
            pltpu.VMEM((rows, columns), jnp.int32),
            pltpu.SMEM((local_freqs,), jnp.int32),
            pltpu.SMEM((local_freqs,), f32),
            pltpu.SMEM(material.shape, f32),
            pltpu.VMEM((1, nsrc), jnp.int32),
            pltpu.VMEM((1, STEPS, nsrc), f32),
            pltpu.VMEM((PLANES, rows, columns), f32),
            pltpu.VMEM((rows, columns), f32),
            pltpu.VMEM((count, PLANES, rows, columns), f32),
            pltpu.VMEM((2, count, rows, columns), f32),
            pltpu.VMEM((1, nsrc), jnp.int32),
            pltpu.VMEM((1, STEPS, nsrc), f32),
            pltpu.VMEM((2, PLANES, rows_all, columns), f32),
            pltpu.VMEM((2, rows_all, columns), f32),
            pltpu.VMEM((STEPS * rows_all, nsrc), f32),
            pltpu.VMEM((2, STEPS * rows_all, wide), f32),
            pltpu.VMEM((local_freqs * rows_all, 2 * STEPS * rows_all), jnp.bfloat16),
            pltpu.VMEM((2, STEPS * rows_all, wide), f32),
            pltpu.VMEM((half, 4 * rows_all, columns), jnp.bfloat16),
            pltpu.VMEM((half, 4 * rows_all, columns), jnp.bfloat16),
            pltpu.VMEM((5, rows_all, columns), f32),
            pltpu.VMEM((count, rows_all // count, columns), f32),
            pltpu.VMEM((count, rows_all // count, columns), f32),
            dma, dma, dma((2,)), dma((2,)), dma((2,)), dma((2,)),
            dma, dma, dma, dma, dma((2,)), dma((7,)),
        ],
        compiler_params=pltpu.CompilerParams(collective_id=0, has_side_effects=True),
    )(fields, material_ids, freq_index, freq_weight, material, source_cells, wavelets, spectra)
    return tuple(pl.pallas_call(
        deliver,
        out_shape=(
            jax.ShapeDtypeStruct(fields.shape, f32),
            jax.ShapeDtypeStruct(spectra.shape, f32),
            jax.ShapeDtypeStruct((rows_all // count, columns), f32),
        ),
        in_specs=[vmem, vmem, vmem],
        out_specs=(anywhere, anywhere, anywhere),
        scratch_shapes=[dma((PIECES + 2,))],
    )(*[pltpu.with_memory_space_constraint(x, pltpu.VMEM) for x in results]))


def solution(mesh):
    return jax.shard_map(
        local,
        mesh=mesh,
        in_specs=(
            P("role", None, "freq", "space"),
            P("role", "freq", None, None, "space"),
            P("freq"),
            P("freq"),
            P("freq", "space"),
            P(),
            P("role", None),
            P("role", None, None),
        ),
        out_specs=(
            P("role", None, "freq", "space"),
            P("role", "freq", None, None, "space"),
            P(("role", "freq"), "space"),
        ),
        check_vma=False,
    )
```
